128 devices in a mesh: tower: 2 (over core), shard: 64 (over y, x, z).
Axes of the slice: x: 4, y: 4, z: 4, core: 2. Of those that a mesh axis runs over, the one named last changes fastest.
Arguments:
- embeds: bfloat16 [2, 131072, 768], P('tower', 'shard'), may hold values from -6 to 6
- pairs: int32 [512, 12], replicated, may hold values from -1 to 1023, as said below
- counts: int32 [512], replicated, may hold values from 1 to 12, as said below
Outputs:
- grads: bfloat16 [2, 131072, 768], P('tower', 'shard')
- stats: float32 [2, 131072], P('tower', 'shard')
The draws below stay inside these ranges and needn't reach their ends.
Inputs may be any that keep to these rules, and one draw needn't show every extreme that they name: `pairs`: entries k < counts[t] are image block numbers, later entries are -1. The listed blocks of all 8 text blocks of one index of shard lie in image rows held by different indices of shard, none of them the same index as the text blocks. The counts of the 8 text blocks of one index of shard add up to at most 63.
All inputs are finite; a program needn't handle non-finite values.
Results may differ from the reference program's by a relative error of at most 0.0038.
Values may be sent and summed in bfloat16 or wider, within the bound.
A program may use at most 128 MiB of HBM per device.

```python
import math
import jax
import jax.numpy as jnp
from jax import lax

D = 768
TXT_BLOCK = 256
IMG_BLOCK = 128
NEG_MAX = 12
TB_DEV = 8
IB_DEV = 16
TBLK = 512
ROWS = 131072


def pair_tables(key):
    base_key = jax.random.fold_in(key, 11)
    keys = jax.random.split(base_key, 6)
    device_count = TBLK // TB_DEV
    level = jax.random.randint(keys[0], (device_count,), 0, 4)
    reach = level * level + 1
    raw = 1 + jax.random.randint(keys[1], (device_count, TB_DEV), 0, 65536) * reach[:, None] // 65536
    raw = jnp.minimum(raw, NEG_MAX)
    heavy_device = jax.random.randint(keys[2], (), 0, device_count)
    heavy_block = jax.random.randint(keys[3], (), 0, TB_DEV)
    device_ids = jnp.arange(device_count)[:, None]
    block_ids = jnp.arange(TB_DEV)[None, :]
    raw = jnp.where(device_ids == heavy_device, jnp.where(block_ids == heavy_block, NEG_MAX, 1), raw)
    ends = jnp.minimum(jnp.cumsum(raw, axis=1), device_count - TB_DEV + block_ids)
    starts = jnp.concatenate([jnp.zeros((device_count, 1), ends.dtype), ends[:, :-1]], axis=1)
    list_sizes = ends - starts
    ranking = jax.random.randint(keys[4], (device_count, device_count), 0, 1 << 20) * device_count + jnp.arange(device_count)[None, :]
    ranking = jnp.where(jnp.eye(device_count, dtype=bool), (1 << 20) * device_count + device_count, ranking)
    order = jnp.argsort(ranking, axis=1).astype(jnp.int32)
    slot_index = starts[:, :, None] + jnp.arange(NEG_MAX)[None, None, :]
    slot_index = jnp.minimum(slot_index, device_count - 1).astype(jnp.int32)
    source_dev = jnp.take_along_axis(order, slot_index.reshape(device_count, TB_DEV * NEG_MAX), axis=1).reshape(device_count, TB_DEV, NEG_MAX)
    local_block = jax.random.randint(keys[5], (device_count, TB_DEV, NEG_MAX), 0, IB_DEV)
    listed = jnp.arange(NEG_MAX)[None, None, :] < list_sizes[:, :, None]
    block_lists = jnp.where(listed, source_dev * IB_DEV + local_block, -1)
    return (block_lists.reshape(TBLK, NEG_MAX).astype(jnp.int32), list_sizes.reshape(TBLK).astype(jnp.int32))


def draw_pairs(key, part):
    return pair_tables(key)[0]


def draw_counts(key, part):
    return pair_tables(key)[1]


def draw_embeds(key, part):
    keys = jax.random.split(jax.random.fold_in(key, 5), 2)
    shape = (2, ROWS, D)
    row_scale = jnp.exp(jax.random.uniform(keys[0], (2, ROWS, 1), jnp.float32, math.log(0.35), math.log(1.6)))
    base = jax.random.normal(keys[1], shape, jnp.float32)
    values = base * row_scale
    return jnp.clip(values, -6.0, 6.0).astype(jnp.bfloat16)


def setup_inputs(seed: int = 0) -> dict:
    arg_keys = jax.random.split(jax.random.key(seed), 4)
    embeds = draw_embeds(jax.random.fold_in(arg_keys[3], 71), 0)
    pairs = draw_pairs(jax.random.fold_in(arg_keys[3], 71), 0)
    counts = draw_counts(jax.random.fold_in(arg_keys[3], 71), 0)
    return dict(embeds=embeds, pairs=pairs, counts=counts)


def reference(embeds, pairs, counts):
    image_rows = embeds[0]
    text_rows = embeds[1]
    row_count = image_rows.shape[0]
    features = image_rows.shape[1]
    image_total = row_count // IMG_BLOCK
    per_text = TXT_BLOCK // IMG_BLOCK
    score_factor = 3.0 / math.sqrt(D)
    image_groups = image_rows.reshape(image_total, IMG_BLOCK, features)

    def per_block(state_pair, inputs):
        image_accum, column_mass = state_pair
        block_index, block_list, list_size = inputs
        first_row = (block_index * TXT_BLOCK).astype(jnp.int32)
        text_block = lax.dynamic_slice_in_dim(text_rows, first_row, TXT_BLOCK, 0)
        paired = lax.dynamic_slice_in_dim(image_rows, first_row, TXT_BLOCK, 0)
        listed = jnp.arange(NEG_MAX, dtype=jnp.int32) < list_size
        block_ids = jnp.where(listed, block_list, 0).astype(jnp.int32)
        key_rows = image_groups[block_ids].reshape(NEG_MAX * IMG_BLOCK, features)
        positive_scores = jnp.dot(text_block, paired.T, preferred_element_type=jnp.float32) * score_factor
        negative_scores = jnp.dot(text_block, key_rows.T, preferred_element_type=jnp.float32) * score_factor
        columns = jnp.repeat(listed, IMG_BLOCK)
        negative_scores = jnp.where(columns[None, :], negative_scores, -jnp.inf)
        running_max = jnp.maximum(lax.optimization_barrier(jnp.max(positive_scores, axis=1)), lax.optimization_barrier(jnp.max(negative_scores, axis=1)))
        sum_exp = lax.optimization_barrier(jnp.sum(jnp.exp(positive_scores - running_max[:, None]), axis=1)) + lax.optimization_barrier(jnp.sum(jnp.exp(negative_scores - running_max[:, None]), axis=1))
        log_total = running_max + jnp.log(sum_exp)
        row_loss = log_total - jnp.diagonal(positive_scores)
        weight_pos = jnp.exp(positive_scores - log_total[:, None]).astype(jnp.bfloat16)
        weight_neg = jnp.where(columns[None, :], jnp.exp(negative_scores - log_total[:, None]), 0.0).astype(jnp.bfloat16)
        text_grad = jnp.dot(weight_pos, paired, preferred_element_type=jnp.float32) + jnp.dot(weight_neg, key_rows, preferred_element_type=jnp.float32) - paired.astype(jnp.float32)
        positive_part = jnp.dot(weight_pos.T, text_block, preferred_element_type=jnp.float32)
        positive_mass = lax.optimization_barrier(jnp.sum(weight_pos.astype(jnp.float32), axis=0))
        negative_part = jnp.dot(weight_neg.T, text_block, preferred_element_type=jnp.float32).reshape(NEG_MAX, IMG_BLOCK, features).astype(jnp.bfloat16)
        negative_mass = lax.optimization_barrier(jnp.sum(weight_neg.astype(jnp.float32), axis=0)).reshape(NEG_MAX, IMG_BLOCK).astype(jnp.bfloat16)
        negative_part, negative_mass = lax.optimization_barrier((negative_part, negative_mass))
        target = jnp.where(listed, block_list, image_total).astype(jnp.int32)
        image_accum = image_accum.at[target].add(negative_part.astype(jnp.float32), mode='drop')
        column_mass = column_mass.at[target].add(negative_mass.astype(jnp.float32), mode='drop')
        own_blocks = (block_index * per_text + jnp.arange(per_text, dtype=jnp.int32)).astype(jnp.int32)
        image_accum = image_accum.at[own_blocks].add(positive_part.reshape(per_text, IMG_BLOCK, features))
        column_mass = column_mass.at[own_blocks].add(positive_mass.reshape(per_text, IMG_BLOCK))
        return ((image_accum, column_mass), (text_grad, row_loss))
    start_state = (jnp.zeros((image_total, IMG_BLOCK, features), jnp.float32), jnp.zeros((image_total, IMG_BLOCK), jnp.float32))
    block_numbers = jnp.arange(pairs.shape[0], dtype=jnp.int32)
    final_state, outputs = lax.scan(per_block, start_state, (block_numbers, pairs, counts))
    image_accum, column_mass = final_state
    text_grads, row_losses = outputs
    text_grad = text_grads.reshape(row_count, features).astype(jnp.bfloat16)
    image_grad = (image_accum.reshape(row_count, features) - text_rows.astype(jnp.float32)).astype(jnp.bfloat16)
    stats = jnp.stack([column_mass.reshape(row_count), row_losses.reshape(row_count)])
    return (jnp.stack([image_grad, text_grad]), stats)
```

```python
import functools
import math

import jax
import jax.numpy as jnp
from jax import lax
from jax.experimental import pallas as pl
from jax.experimental.pallas import tpu as pltpu
from jax.sharding import PartitionSpec as P

MESH = pl.DeviceIdType.MESH
TXT = 256
IMG = 128
TB = 8
IB = 16
SIDE = 4
CHIPS = 64
SLOTS = 32
STEP = 45
STEP_INV = 37
NT = (((1,), (1,)), ((), ()))
TN = (((0,), (0,)), ((), ()))


def hop_of(p):
    return (p * STEP) % CHIPS


def moved(chip, hop, sign):
    y = (chip // 16 + sign * (hop // 16) + SIDE) % SIDE
    x = ((chip // 4) % SIDE + sign * ((hop // 4) % SIDE) + SIDE) % SIDE
    z = (chip % SIDE + sign * (hop % SIDE) + SIDE) % SIDE
    return y * 16 + x * 4 + z


def kernel(
    factor,
    lister_ref,
    wanted_ref,
    entry_ref,
    own_ref,
    text_ref,
    blk16_ref,
    blk8_ref,
    out_ref,
    stat_ref,
    ibuf,
    xbuf,
    recv,
    send,
    ret,
    escore,
    wbuf,
    mst,
    tg,
    img,
    acc,
    lse_ref,
    st,
    pst,
    mneg,
    mret,
    pmass,
    fs,
    fr,
    rs,
    rr,
    ms,
    mr,
    ts,
    tr,
    gs,
    gr,
    one,
):
    t = lax.axis_index("tower")
    s = lax.axis_index("shard")
    other = 1 - t

    def dev(tower, chip):
        return {"tower": tower, "shard": chip}

    def fwd(j):
        p = 2 * j + t
        return pltpu.make_async_remote_copy(
            src_ref=send.at[j],
            dst_ref=recv.at[j],
            send_sem=fs.at[j],
            recv_sem=fr.at[j],
            device_id=dev(t, moved(s, hop_of(p), 1)),
            device_id_type=MESH,
        )

    def back(j):
        p = 2 * j + t
        return pltpu.make_async_remote_copy(
            src_ref=send.at[j],
            dst_ref=ret.at[p],
            send_sem=rs.at[j],
            recv_sem=rr.at[p],
            device_id=dev(0, moved(s, hop_of(p), -1)),
            device_id_type=MESH,
        )

    def back_mass(j):
        p = 2 * j + t
        return pltpu.make_async_remote_copy(
            src_ref=mneg.at[j],
            dst_ref=mret.at[p],
            send_sem=ms.at[j],
            recv_sem=mr.at[p],
            device_id=dev(0, moved(s, hop_of(p), -1)),
            device_id_type=MESH,
        )

    def arrived(p):
        return pltpu.make_async_remote_copy(
            src_ref=ret.at[p],
            dst_ref=ret.at[p],
            send_sem=rs.at[0],
            recv_sem=rr.at[p],
            device_id=dev(1, s),
            device_id_type=MESH,
        )

    def arrived_mass(p):
        return pltpu.make_async_remote_copy(
            src_ref=mret.at[p],
            dst_ref=mret.at[p],
            send_sem=ms.at[0],
            recv_sem=mr.at[p],
            device_id=dev(1, s),
            device_id_type=MESH,
        )

    def give(src, dst, ssem, rsem):
        return pltpu.make_async_remote_copy(
            src_ref=src,
            dst_ref=dst,
            send_sem=ssem,
            recv_sem=rsem,
            device_id=dev(other, s),
            device_id_type=MESH,
        )

    barrier = pltpu.get_barrier_semaphore()

    @pl.when(t == 0)
    def _():
        load = pltpu.make_async_copy(own_ref, ibuf, one.at[0])
        load.start()
        recv[0] = jnp.zeros((IMG, recv.shape[2]), recv.dtype)
        ret[0] = jnp.zeros((IMG, ret.shape[2]), ret.dtype)
        mret[0] = jnp.zeros((8, IMG), mret.dtype)
        wbuf[0] = jnp.zeros((IMG, TXT), wbuf.dtype)

        def greet(p, carry):
            pl.semaphore_signal(
                barrier,
                inc=1,
                device_id=dev(p % 2, moved(s, hop_of(p), 1)),
                device_id_type=MESH,
            )
            return carry

        lax.fori_loop(1, CHIPS, greet, 0)
        load.wait()

    @pl.when(t == 1)
    def _():
        load = pltpu.make_async_copy(text_ref, xbuf, one.at[0])
        load.start()

        def greet(j, carry):
            chip = moved(s, hop_of(2 * j + 1), 1)
            for tower in range(2):
                pl.semaphore_signal(
                    barrier, inc=1, device_id=dev(tower, chip), device_id_type=MESH
                )
            return carry

        lax.fori_loop(0, SLOTS, greet, 0)
        load.wait()

    pl.semaphore_signal(barrier, inc=1, device_id=dev(other, s), device_id_type=MESH)

    @pl.when(t == 0)
    def _():
        pl.semaphore_wait(barrier, 64)
        give(ibuf, ibuf, one.at[1], one.at[2]).start()

    @pl.when(t == 1)
    def _():
        pl.semaphore_wait(barrier, 65)
        give(xbuf, xbuf, one.at[1], one.at[3]).start()
        give(ibuf, ibuf, one.at[1], one.at[2]).wait_recv()

    def pack(j, carry):
        @pl.when(j < SLOTS)
        def _():
            chip = moved(s, hop_of(2 * j + t), 1)
            send[jnp.minimum(j, SLOTS - 1)] = ibuf[jnp.maximum(wanted_ref[chip], 0)]

        @pl.when(2 * j + t >= 3)
        def _():
            fwd(j - 1).start()

        return carry

    lax.fori_loop(0, SLOTS + 1, pack, 0)

    @pl.when(t == 0)
    def _():
        give(xbuf, xbuf, one.at[1], one.at[3]).wait_recv()

    rows8 = lax.broadcasted_iota(jnp.int32, (TB, TXT), 0)
    sub = lax.broadcasted_iota(jnp.int32, (IMG, TXT), 0)
    lane = lax.broadcasted_iota(jnp.int32, (IMG, TXT), 1)
    on_diag = lane == sub + t * IMG

    def scores(keys, block):
        got = lax.dot_general(
            keys, xbuf[block], NT, preferred_element_type=jnp.float32
        )
        return got * factor

    def keep(slot, val):
        top = jnp.max(val, axis=0, keepdims=True)
        ex = jnp.exp(val - top)
        escore[slot] = ex
        mst[slot] = top
        return top, jnp.sum(ex, axis=0, keepdims=True)

    def positive(block, carry):
        big, total, diag = carry
        val = scores(ibuf[2 * block + t], block)
        top, part = keep(SLOTS + block, val)
        here = rows8 == block
        on = jnp.sum(jnp.where(on_diag, val, 0.0), axis=0, keepdims=True)
        return (
            jnp.where(here, top, big),
            jnp.where(here, part, total),
            jnp.where(here, on, diag),
        )

    zero = jnp.zeros((TB, TXT), jnp.float32)
    big, total, diag = lax.fori_loop(0, TB, positive, (zero, zero, zero))

    def listed(j, carry):
        big, total = carry
        fwd(j).wait_recv()
        block = lister_ref[moved(s, hop_of(2 * j + t), -1)]
        val = scores(recv[j], jnp.maximum(block, 0))
        top, part = keep(j, val)
        here = rows8 == block
        new = jnp.where(here, jnp.maximum(big, top), big)
        total = total * jnp.exp(big - new) + jnp.where(
            here, part * jnp.exp(top - new), 0.0
        )
        return new, total

    big, total = lax.fori_loop(1 - t, SLOTS, listed, (big, total))

    st[0] = big
    st[1] = total
    st[2] = diag
    share = give(st, pst, one.at[4], one.at[5])
    share.start()
    share.wait()
    big_o = pst[0]
    new = jnp.maximum(big, big_o)
    lse = new + jnp.log(total * jnp.exp(big - new) + pst[1] * jnp.exp(big_o - new))
    lse_ref[...] = lse
    loss = lse - (diag + pst[2])

    ones = jnp.ones((8, TXT), jnp.bfloat16)

    def column_mass(weight):
        return lax.dot_general(ones, weight, NT, preferred_element_type=jnp.float32)

    def depart(j):
        back(j).start()
        back_mass(j).start()

    def answer(j, carry):
        fwd(j).wait_send()
        block = lister_ref[moved(s, hop_of(2 * j + t), -1)]
        held = jnp.maximum(block, 0)
        scale = jnp.exp(mst[j] - lse_ref[pl.ds(held, 1), :])
        scale = jnp.where(block >= 0, scale, 0.0)
        weight = (escore[j] * scale).astype(jnp.bfloat16)
        wbuf[j] = weight
        send[j] = jnp.dot(
            weight, xbuf[held], preferred_element_type=jnp.float32
        ).astype(jnp.bfloat16)
        mneg[j] = column_mass(weight)

        @pl.when(2 * j + t >= 3)
        def _():
            depart(j - 1)

        return carry

    lax.fori_loop(1 - t, SLOTS, answer, 0)

    def answer_own(block, carry):
        slot = SLOTS + block
        scale = jnp.exp(mst[slot] - lse_ref[pl.ds(block, 1), :])
        weight = (escore[slot] * scale).astype(jnp.bfloat16)
        wbuf[slot] = weight
        part = jnp.dot(weight, xbuf[block], preferred_element_type=jnp.float32)
        mine = xbuf[block, pl.ds(pl.multiple_of(t * IMG, IMG), IMG), :]
        img[2 * block + t] = part - mine.astype(jnp.float32)
        pmass[block + TB * t] = column_mass(weight)
        return carry

    depart(SLOTS - 1)
    lax.fori_loop(0, TB, answer_own, 0)

    def give_image(block):
        return give(
            img.at[2 * block + 1], img.at[2 * block + 1], gs.at[block], gr.at[block]
        )

    give_mass = give(pmass.at[pl.ds(TB, TB)], pmass.at[pl.ds(TB, TB)], one.at[6], one.at[7])

    @pl.when(t == 1)
    def _():
        for block in range(TB):
            give_image(block).start()
        give_mass.start()

    def text(block):
        acc[...] = lax.dot_general(
            wbuf[SLOTS + block], ibuf[2 * block + t], TN, preferred_element_type=jnp.float32
        )

        def add(k, carry):
            ws, ks = [], []
            for half in range(2):
                slot = entry_ref[block * 12 + 2 * k + half]
                at = jnp.maximum(slot, 0)
                w = wbuf[at]
                ws.append(jnp.where(slot >= 0, w, jnp.zeros_like(w)))
                ks.append(recv[at])
            acc[...] += lax.dot_general(
                jnp.concatenate(ws, axis=0),
                jnp.concatenate(ks, axis=0),
                TN,
                preferred_element_type=jnp.float32,
            )
            return carry

        lax.fori_loop(0, 6, add, 0)
        rows = pl.ds(pl.multiple_of(t * IMG, IMG), IMG)
        acc[rows, :] = acc[rows, :] - ibuf[2 * block + t].astype(jnp.float32)

    def give_text(block):
        return give(tg.at[block], tg.at[block], ts.at[block], tr.at[block])

    @pl.when(t == 0)
    def _():
        def run(block, carry):
            text(block)
            tg[block] = acc[...]

            @pl.when(block >= 1)
            def _():
                give_text(block - 1).start()

            return carry

        lax.fori_loop(0, TB, run, 0)

        for block in range(TB):
            give_image(block).wait_recv()
        give_text(TB - 1).start()
        give_mass.wait_recv()
        r = lax.broadcasted_iota(jnp.int32, (TXT, TXT), 0)
        c = lax.broadcasted_iota(jnp.int32, (TXT, TXT), 1)
        same_row = (r % IB) == (c % IB)

        for q in range(4):
            for k in range(16):
                if q + k > 0:
                    arrived(16 * q + k).wait_recv()
            pick = jnp.where(
                same_row & (r // IB == blk16_ref[pl.ds(q, 1), :]), 1.0, 0.0
            ).astype(jnp.bfloat16)

            def gather(g, carry):
                rows = pl.ds(pl.multiple_of(g * 16, 16), 16)
                part = ret[pl.ds(16 * q, 16), rows, :].reshape(TXT, ret.shape[2])
                got = jnp.dot(pick, part, preferred_element_type=jnp.float32)
                got = img[:, rows, :] + got.reshape(IB, 16, ret.shape[2])
                if q < 3:
                    img[:, rows, :] = got
                else:
                    out_ref[:, rows, :] = got.astype(jnp.bfloat16)
                return carry

            lax.fori_loop(0, 8, gather, 0)

        for p in range(1, CHIPS):
            arrived_mass(p).wait_recv()
        b = lax.broadcasted_iota(jnp.int32, (IB, 8 * CHIPS), 0)
        k8 = lax.broadcasted_iota(jnp.int32, (IB, 8 * CHIPS), 1)
        pick8 = jnp.where((b == blk8_ref[...]) & (k8 % 8 == 0), 1.0, 0.0).astype(
            jnp.bfloat16
        )
        mass = jnp.dot(
            pick8,
            mret[...].reshape(8 * CHIPS, IMG).astype(jnp.bfloat16),
            preferred_element_type=jnp.float32,
        )
        stat_ref[...] = mass
        for block in range(TB):
            for half in range(2):
                at = 2 * block + half
                stat_ref[at : at + 1, :] += pmass[block + TB * half, 0:1, :]
        for block in range(TB):
            give_text(block).wait_send()

    @pl.when(t == 1)
    def _():
        def run(block, carry):
            text(block)
            give_text(block).wait_recv()
            done = (acc[...] + tg[block]).astype(jnp.bfloat16)
            out_ref[pl.ds(2 * block, 2)] = done.reshape(2, IMG, done.shape[1])
            return carry

        lax.fori_loop(0, TB, run, 0)
        for block in range(TB):
            for half in range(2):
                at = 2 * block + half
                stat_ref[at : at + 1, :] = loss[
                    block : block + 1, half * IMG : (half + 1) * IMG
                ]
        for block in range(TB):
            give_image(block).wait_send()
        give_mass.wait_send()

    give(ibuf, ibuf, one.at[1], one.at[2]).wait_send()

    def drain(j, carry):
        back(j).wait_send()
        back_mass(j).wait_send()
        return carry

    lax.fori_loop(1 - t, SLOTS, drain, 0)


def body(embeds, pairs, counts):
    rows = embeds.shape[1]
    features = embeds.shape[2]
    slots = pairs.shape[1]
    t = lax.axis_index("tower")
    s = lax.axis_index("shard")
    listed = jnp.arange(slots, dtype=jnp.int32)[None, :] < counts[:, None]
    source = jnp.where(listed, pairs // IB, -1)
    local = pairs % IB

    hit = source.reshape(CHIPS, TB * slots) == s
    wanted = jnp.max(jnp.where(hit, local.reshape(CHIPS, TB * slots), -1), axis=1)
    mine = lax.dynamic_slice_in_dim(source, s * TB, TB, 0)
    chips = jnp.arange(CHIPS, dtype=jnp.int32)
    block = lax.broadcasted_iota(jnp.int32, (CHIPS, TB, slots), 1)
    lister = jnp.max(
        jnp.where(mine[None] == chips[:, None, None], block, -1), axis=(1, 2)
    )
    hop = (
        ((s // 16 - mine // 16) % SIDE) * 16
        + ((s // 4 - mine // 4) % SIDE) * 4
        + (s - mine) % SIDE
    )
    step = (hop * STEP_INV) % CHIPS
    entry = jnp.where((mine >= 0) & (step % 2 == t), step // 2, -1).reshape(TB * slots)
    target = moved(s, hop_of(chips), 1)
    by_step = jnp.max(
        jnp.where(target[:, None] == chips[None, :], wanted[None, :], -1), axis=1
    )
    blk16 = jnp.broadcast_to(by_step[:, None], (CHIPS, 16)).reshape(4, 16 * 16)
    blk8 = jnp.broadcast_to(by_step[:, None], (CHIPS, 8)).reshape(1, 8 * CHIPS)

    smem = pl.BlockSpec(memory_space=pltpu.SMEM)
    vmem = pl.BlockSpec(memory_space=pltpu.VMEM)
    bf16, f32 = jnp.bfloat16, jnp.float32
    dma = pltpu.SemaphoreType.DMA
    grads, stats = pl.pallas_call(
        functools.partial(kernel, 3.0 / math.sqrt(features)),
        out_shape=(
            jax.ShapeDtypeStruct((IB, IMG, features), bf16),
            jax.ShapeDtypeStruct((IB, IMG), f32),
        ),
        in_specs=[smem] * 3 + [pl.BlockSpec(memory_space=pl.ANY)] * 2 + [vmem] * 2,
        out_specs=(vmem, vmem),
        scratch_shapes=[
            pltpu.VMEM((IB, IMG, features), bf16),
            pltpu.VMEM((TB, TXT, features), bf16),
            pltpu.VMEM((SLOTS, IMG, features), bf16),
            pltpu.VMEM((SLOTS, IMG, features), bf16),
            pltpu.VMEM((CHIPS, IMG, features), bf16),
            pltpu.VMEM((SLOTS + TB, IMG, TXT), f32),
            pltpu.VMEM((SLOTS + TB, IMG, TXT), bf16),
            pltpu.VMEM((SLOTS + TB, 1, TXT), f32),
            pltpu.VMEM((TB, TXT, features), f32),
            pltpu.VMEM((IB, IMG, features), f32),
            pltpu.VMEM((TXT, features), f32),
            pltpu.VMEM((TB, TXT), f32),
            pltpu.VMEM((3, TB, TXT), f32),
            pltpu.VMEM((3, TB, TXT), f32),
            pltpu.VMEM((SLOTS, 8, IMG), f32),
            pltpu.VMEM((CHIPS, 8, IMG), f32),
            pltpu.VMEM((2 * TB, 8, IMG), f32),
            dma((SLOTS,)),
            dma((SLOTS,)),
            dma((SLOTS,)),
            dma((CHIPS,)),
            dma((SLOTS,)),
            dma((CHIPS,)),
            dma((TB,)),
            dma((TB,)),
            dma((TB,)),
            dma((TB,)),
            dma((8,)),
        ],
        compiler_params=pltpu.CompilerParams(
            collective_id=0, has_side_effects=True, vmem_limit_bytes=67_000_000
        ),
    )(
        lister,
        wanted,
        entry,
        embeds[0].reshape(IB, IMG, features),
        embeds[0].reshape(TB, TXT, features),
        blk16,
        blk8,
    )
    return grads.reshape(1, rows, features), stats.reshape(1, rows)


def solution(mesh):
    placed = (P("tower", "shard", None), P(), P())
    return jax.shard_map(
        body,
        mesh=mesh,
        in_specs=placed,
        out_specs=(P("tower", "shard", None), P("tower", "shard")),
        check_vma=False,
    )
```

```python
import functools
import math

import jax
import jax.numpy as jnp
from jax import lax
from jax.experimental import pallas as pl
from jax.experimental.pallas import tpu as pltpu
from jax.sharding import PartitionSpec as P

MESH = pl.DeviceIdType.MESH
TXT = 256
IMG = 128
TB = 8
IB = 16
SIDE = 4
CHIPS = 64
SLOTS = 32
GROUP = 4
STEP = 45
STEP_INV = 37
NT = (((1,), (1,)), ((), ()))
TN = (((0,), (0,)), ((), ()))


def hop_of(p):
    return lax.rem(p * STEP, CHIPS)


def moved(chip, hop, sign):
    div, rem = lax.div, lax.rem
    y = rem(div(chip, 16) + sign * div(hop, 16) + SIDE, SIDE)
    x = rem(rem(div(chip, 4), SIDE) + sign * rem(div(hop, 4), SIDE) + SIDE, SIDE)
    z = rem(rem(chip, SIDE) + sign * rem(hop, SIDE) + SIDE, SIDE)
    return y * 16 + x * 4 + z


def kernel(
    factor,
    lister_ref,
    wanted_ref,
    entry_ref,
    image_own,
    image_got,
    text_own,
    text_got,
    out_ref,
    stat_ref,
    ibuf,
    xbuf,
    recv,
    send,
    ret,
    escore,
    wbuf,
    mst,
    tg,
    img,
    acc,
    lse_ref,
    st,
    pst,
    mneg,
    mret,
    pmass,
    fs,
    fr,
    rs,
    rr,
    ms,
    mr,
    ts,
    tr,
    gs,
    gr,
    one,
    put,
):
    t = lax.axis_index("tower")
    s = lax.axis_index("shard")
    other = 1 - t

    def dev(tower, chip):
        return {"tower": tower, "shard": chip}

    def fwd(j):
        p = 2 * j + t
        return pltpu.make_async_remote_copy(
            src_ref=send.at[j],
            dst_ref=recv.at[j],
            send_sem=fs.at[j],
            recv_sem=fr.at[j],
            device_id=dev(t, moved(s, hop_of(p), 1)),
            device_id_type=MESH,
        )

    def back(j):
        p = 2 * j + t
        return pltpu.make_async_remote_copy(
            src_ref=send.at[j],
            dst_ref=ret.at[p],
            send_sem=rs.at[j],
            recv_sem=rr.at[p],
            device_id=dev(0, moved(s, hop_of(p), -1)),
            device_id_type=MESH,
        )

    def back_mass(j):
        p = 2 * j + t
        return pltpu.make_async_remote_copy(
            src_ref=mneg.at[j],
            dst_ref=mret.at[p],
            send_sem=ms.at[j],
            recv_sem=mr.at[p],
            device_id=dev(0, moved(s, hop_of(p), -1)),
            device_id_type=MESH,
        )

    def arrived(p):
        return pltpu.make_async_remote_copy(
            src_ref=ret.at[p],
            dst_ref=ret.at[p],
            send_sem=rs.at[0],
            recv_sem=rr.at[p],
            device_id=dev(1, s),
            device_id_type=MESH,
        )

    def arrived_mass(p):
        return pltpu.make_async_remote_copy(
            src_ref=mret.at[p],
            dst_ref=mret.at[p],
            send_sem=ms.at[0],
            recv_sem=mr.at[p],
            device_id=dev(1, s),
            device_id_type=MESH,
        )

    def give(src, dst, ssem, rsem):
        return pltpu.make_async_remote_copy(
            src_ref=src,
            dst_ref=dst,
            send_sem=ssem,
            recv_sem=rsem,
            device_id=dev(other, s),
            device_id_type=MESH,
        )

    def loads(image, words, act):
        getattr(pltpu.make_async_copy(image, ibuf, one.at[0]), act)()
        getattr(pltpu.make_async_copy(words, xbuf, one.at[1]), act)()

    barrier = pltpu.get_barrier_semaphore()

    @pl.when(t == 0)
    def _():
        loads(image_own, text_got, "start")
        recv[0] = jnp.zeros((IMG, recv.shape[2]), recv.dtype)
        ret[0] = jnp.zeros((IMG, ret.shape[2]), ret.dtype)
        mret[0] = jnp.zeros((1, IMG), mret.dtype)
        wbuf[0] = jnp.zeros((IMG, TXT), wbuf.dtype)

        def greet(p, carry):
            pl.semaphore_signal(
                barrier,
                inc=1,
                device_id=dev(lax.rem(p, 2), moved(s, hop_of(p), 1)),
                device_id_type=MESH,
            )
            return carry

        lax.fori_loop(1, CHIPS, greet, 0)

    @pl.when(t == 1)
    def _():
        loads(image_got, text_own, "start")

        def greet(j, carry):
            chip = moved(s, hop_of(2 * j + 1), 1)
            for tower in range(2):
                pl.semaphore_signal(
                    barrier, inc=1, device_id=dev(tower, chip), device_id_type=MESH
                )
            return carry

        lax.fori_loop(0, SLOTS, greet, 0)

    pl.semaphore_signal(barrier, inc=1, device_id=dev(other, s), device_id_type=MESH)

    @pl.when(t == 0)
    def _():
        loads(image_own, text_got, "wait")
        pl.semaphore_wait(barrier, 64)

    @pl.when(t == 1)
    def _():
        loads(image_got, text_own, "wait")
        pl.semaphore_wait(barrier, 65)

    def pack(j, carry):
        @pl.when(j < SLOTS)
        def _():
            chip = moved(s, hop_of(2 * j + t), 1)
            send[jnp.minimum(j, SLOTS - 1)] = ibuf[jnp.maximum(wanted_ref[chip], 0)]

        @pl.when(2 * j + t >= 3)
        def _():
            fwd(j - 1).start()

        return carry

    lax.fori_loop(0, SLOTS + 1, pack, 0)

    rows8 = lax.broadcasted_iota(jnp.int32, (TB, TXT), 0)
    sub = lax.broadcasted_iota(jnp.int32, (IMG, TXT), 0)
    lane = lax.broadcasted_iota(jnp.int32, (IMG, TXT), 1)
    on_diag = lane == sub + t * IMG

    def scores(keys, block):
        got = lax.dot_general(
            keys, xbuf[block], NT, preferred_element_type=jnp.float32
        )
        return got * factor

    def keep(slot, val):
        top = jnp.max(val, axis=0, keepdims=True)
        ex = jnp.exp(val - top)
        escore[slot] = ex
        mst[slot] = top
        return top, jnp.sum(ex, axis=0, keepdims=True)

    def positive(block, carry):
        big, total, diag = carry
        val = scores(ibuf[2 * block + t], block)
        top, part = keep(SLOTS + block, val)
        here = rows8 == block
        on = jnp.sum(jnp.where(on_diag, val, 0.0), axis=0, keepdims=True)
        return (
            jnp.where(here, top, big),
            jnp.where(here, part, total),
            jnp.where(here, on, diag),
        )

    zero = jnp.zeros((TB, TXT), jnp.float32)
    big, total, diag = lax.fori_loop(0, TB, positive, (zero, zero, zero))

    def listed(group, carry):
        big, total = carry
        got = []
        for k in range(GROUP):
            j = group * GROUP + k

            @pl.when(2 * j + t > 0)
            def _():
                fwd(j).wait_recv()

        for k in range(GROUP):
            j = group * GROUP + k
            block = lister_ref[moved(s, hop_of(2 * j + t), -1)]
            val = scores(recv[j], jnp.maximum(block, 0))
            got.append((block, *keep(j, val)))
        new = big
        for block, top, _ in got:
            new = jnp.where(rows8 == block, jnp.maximum(new, top), new)
        total = total * jnp.exp(big - new)
        for block, top, part in got:
            total += jnp.where(rows8 == block, part * jnp.exp(top - new), 0.0)
        return new, total

    big, total = lax.fori_loop(0, SLOTS // GROUP, listed, (big, total))

    st[0] = big
    st[1] = total
    st[2] = diag
    share = give(st, pst, one.at[4], one.at[5])
    share.start()
    share.wait()
    big_o = pst[0]
    new = jnp.maximum(big, big_o)
    lse = new + jnp.log(total * jnp.exp(big - new) + pst[1] * jnp.exp(big_o - new))
    lse_ref[...] = lse
    loss = lse - (diag + pst[2])

    ones = jnp.ones((8, TXT), jnp.bfloat16)

    def column_mass(weight):
        got = lax.dot_general(ones, weight, NT, preferred_element_type=jnp.float32)
        return got[0:1]

    def depart(j):
        back(j).start()
        back_mass(j).start()

    def answer(j, carry):
        fwd(j).wait_send()
        block = lister_ref[moved(s, hop_of(2 * j + t), -1)]
        held = jnp.maximum(block, 0)
        scale = jnp.exp(mst[j] - lse_ref[pl.ds(held, 1), :])
        scale = jnp.where(block >= 0, scale, 0.0)
        weight = (escore[j] * scale).astype(jnp.bfloat16)
        wbuf[j] = weight
        send[j] = jnp.dot(
            weight, xbuf[held], preferred_element_type=jnp.float32
        ).astype(jnp.bfloat16)
        mneg[j] = column_mass(weight)

        @pl.when(2 * j + t >= 3)
        def _():
            depart(j - 1)

        return carry

    lax.fori_loop(1 - t, SLOTS, answer, 0)

    def answer_own(block, carry):
        slot = SLOTS + block
        scale = jnp.exp(mst[slot] - lse_ref[pl.ds(block, 1), :])
        weight = (escore[slot] * scale).astype(jnp.bfloat16)
        wbuf[slot] = weight
        part = jnp.dot(weight, xbuf[block], preferred_element_type=jnp.float32)
        mine = xbuf[block, pl.ds(pl.multiple_of(t * IMG, IMG), IMG), :]
        img[2 * block + t] = part - mine.astype(jnp.float32)
        pmass[block + TB * t] = column_mass(weight)
        return carry

    depart(SLOTS - 1)
    lax.fori_loop(0, TB, answer_own, 0)

    def give_image(block):
        return give(
            img.at[2 * block + 1], img.at[2 * block + 1], gs.at[block], gr.at[block]
        )

    give_mass = give(pmass.at[pl.ds(TB, TB)], pmass.at[pl.ds(TB, TB)], one.at[6], one.at[7])

    @pl.when(t == 1)
    def _():
        for block in range(TB):
            give_image(block).start()
        give_mass.start()

    def text(block):
        acc[...] = lax.dot_general(
            wbuf[SLOTS + block], ibuf[2 * block + t], TN, preferred_element_type=jnp.float32
        )

        def add(k, carry):
            ws, ks = [], []
            for half in range(2):
                slot = entry_ref[block, 2 * k + half]
                at = jnp.maximum(slot, 0)
                w = wbuf[at]
                ws.append(jnp.where(slot >= 0, w, jnp.zeros_like(w)))
                ks.append(recv[at])
            acc[...] += lax.dot_general(
                jnp.concatenate(ws, axis=0),
                jnp.concatenate(ks, axis=0),
                TN,
                preferred_element_type=jnp.float32,
            )
            return carry

        lax.fori_loop(0, 6, add, 0)
        rows = pl.ds(pl.multiple_of(t * IMG, IMG), IMG)
        acc[rows, :] = acc[rows, :] - ibuf[2 * block + t].astype(jnp.float32)

    def give_text(block):
        return give(tg.at[block], tg.at[block], ts.at[block], tr.at[block])

    @pl.when(t == 0)
    def _():
        def run(block, carry):
            text(block)
            tg[block] = acc[...]

            @pl.when(block >= 1)
            def _():
                give_text(block - 1).start()

            return carry

        lax.fori_loop(0, TB, run, 0)

        for block in range(TB):
            give_image(block).wait_recv()
        give_text(TB - 1).start()
        give_mass.wait_recv()
        r = lax.broadcasted_iota(jnp.int32, (TXT, TXT), 0)
        c = lax.broadcasted_iota(jnp.int32, (TXT, TXT), 1)
        same_row = (r % IB) == (c % IB)
        c1 = lax.broadcasted_iota(jnp.int32, (1, TXT), 1)
        cp = lax.broadcasted_iota(jnp.int32, (1, CHIPS), 1)

        def put_rows(g):
            rows = pl.ds(pl.multiple_of(g * 16, 16), 16)
            return pltpu.make_async_copy(
                ibuf.at[:, rows, :], out_ref.at[:, rows, :], put.at[g]
            )

        def wanted_at(p):
            return wanted_ref[moved(s, hop_of(p), 1)]


        for q in range(4):
            for k in range(16):
                if q + k > 0:
                    arrived(16 * q + k).wait_recv()
            blk16 = jnp.full((1, TXT), -1, jnp.int32)
            for k in range(16):
                blk16 = jnp.where(c1 // 16 == k, wanted_at(16 * q + k), blk16)
            pick = jnp.where(same_row & (r // IB == blk16), 1.0, 0.0).astype(
                jnp.bfloat16
            )

            def gather(g, carry):
                rows = pl.ds(pl.multiple_of(g * 16, 16), 16)
                part = ret[pl.ds(16 * q, 16), rows, :].reshape(TXT, ret.shape[2])
                got = jnp.dot(pick, part, preferred_element_type=jnp.float32)
                got = img[:, rows, :] + got.reshape(IB, 16, ret.shape[2])
                if q < 3:
                    img[:, rows, :] = got
                else:
                    ibuf[:, rows, :] = got.astype(jnp.bfloat16)
                    put_rows(g).start()
                return carry

            lax.fori_loop(0, 8, gather, 0)

        for p in range(1, CHIPS):
            arrived_mass(p).wait_recv()
        b = lax.broadcasted_iota(jnp.int32, (IB, CHIPS), 0)
        blocks = jnp.full((1, CHIPS), -1, jnp.int32)
        for p in range(CHIPS):
            blocks = jnp.where(cp == p, wanted_at(p), blocks)
        mass = jnp.dot(
            jnp.where(b == blocks, 1.0, 0.0).astype(jnp.bfloat16),
            mret[...].reshape(CHIPS, IMG).astype(jnp.bfloat16),
            preferred_element_type=jnp.float32,
        )
        stat_ref[...] = mass
        for block in range(TB):
            for half in range(2):
                at = 2 * block + half
                stat_ref[at : at + 1, :] += pmass[block + TB * half]
        for block in range(TB):
            give_text(block).wait_send()
            put_rows(block).wait()

    @pl.when(t == 1)
    def _():
        def put_block(block):
            rows = pl.ds(2 * block, 2)
            return pltpu.make_async_copy(ibuf.at[rows], out_ref.at[rows], put.at[block])

        def run(block, carry):
            text(block)
            give_text(block).wait_recv()
            done = (acc[...] + tg[block]).astype(jnp.bfloat16)
            ibuf[pl.ds(2 * block, 2)] = done.reshape(2, IMG, done.shape[1])
            put_block(block).start()
            return carry

        lax.fori_loop(0, TB, run, 0)
        for block in range(TB):
            for half in range(2):
                at = 2 * block + half
                stat_ref[at : at + 1, :] = loss[
                    block : block + 1, half * IMG : (half + 1) * IMG
                ]
        for block in range(TB):
            give_image(block).wait_send()
            put_block(block).wait()
        give_mass.wait_send()

    def drain(j, carry):
        back(j).wait_send()
        back_mass(j).wait_send()
        return carry

    lax.fori_loop(1 - t, SLOTS, drain, 0)


def body(embeds, pairs, counts):
    rows = embeds.shape[1]
    features = embeds.shape[2]
    slots = pairs.shape[1]
    t = lax.axis_index("tower")
    s = lax.axis_index("shard")
    listed = jnp.arange(slots, dtype=jnp.int32)[None, :] < counts[:, None]
    source = jnp.where(listed, pairs // IB, -1)
    local = pairs % IB

    hit = source.reshape(CHIPS, TB * slots) == s
    wanted = jnp.max(jnp.where(hit, local.reshape(CHIPS, TB * slots), -1), axis=1)
    mine = lax.dynamic_slice_in_dim(source, s * TB, TB, 0)
    chips = jnp.arange(CHIPS, dtype=jnp.int32)
    block = lax.broadcasted_iota(jnp.int32, (CHIPS, TB, slots), 1)
    lister = jnp.max(
        jnp.where(mine[None] == chips[:, None, None], block, -1), axis=(1, 2)
    )
    hop = (
        ((s // 16 - mine // 16) % SIDE) * 16
        + ((s // 4 - mine // 4) % SIDE) * 4
        + (s - mine) % SIDE
    )
    step = (hop * STEP_INV) % CHIPS
    entry = jnp.where((mine >= 0) & (step % 2 == t), step // 2, -1)
    smem = pl.BlockSpec(memory_space=pltpu.SMEM)
    vmem = pl.BlockSpec(memory_space=pltpu.VMEM)
    bf16, f32 = jnp.bfloat16, jnp.float32
    own = embeds[0]
    got = lax.ppermute(own, "tower", [(0, 1), (1, 0)])
    dma = pltpu.SemaphoreType.DMA
    grads, stats = pl.pallas_call(
        functools.partial(kernel, 3.0 / math.sqrt(features)),
        out_shape=(
            jax.ShapeDtypeStruct((IB, IMG, features), bf16),
            jax.ShapeDtypeStruct((IB, IMG), f32),
        ),
        in_specs=[smem] * 3 + [pl.BlockSpec(memory_space=pl.ANY)] * 4,
        out_specs=(pl.BlockSpec(memory_space=pl.ANY), vmem),
        scratch_shapes=[
            pltpu.VMEM((IB, IMG, features), bf16),
            pltpu.VMEM((TB, TXT, features), bf16),
            pltpu.VMEM((SLOTS, IMG, features), bf16),
            pltpu.VMEM((SLOTS, IMG, features), bf16),
            pltpu.VMEM((CHIPS, IMG, features), bf16),
            pltpu.VMEM((SLOTS + TB, IMG, TXT), f32),
            pltpu.VMEM((SLOTS + TB, IMG, TXT), bf16),
            pltpu.VMEM((SLOTS + TB, 1, TXT), f32),
            pltpu.VMEM((TB, TXT, features), f32),
            pltpu.VMEM((IB, IMG, features), f32),
            pltpu.VMEM((TXT, features), f32),
            pltpu.VMEM((TB, TXT), f32),
            pltpu.VMEM((3, TB, TXT), f32),
            pltpu.VMEM((3, TB, TXT), f32),
            pltpu.VMEM((SLOTS, 1, IMG), f32),
            pltpu.VMEM((CHIPS, 1, IMG), f32),
            pltpu.VMEM((2 * TB, 1, IMG), f32),
            dma((SLOTS,)),
            dma((SLOTS,)),
            dma((SLOTS,)),
            dma((CHIPS,)),
            dma((SLOTS,)),
            dma((CHIPS,)),
            dma((TB,)),
            dma((TB,)),
            dma((TB,)),
            dma((TB,)),
            dma((8,)),
            dma((TB,)),
        ],
        compiler_params=pltpu.CompilerParams(
            collective_id=0, has_side_effects=True, vmem_limit_bytes=67_000_000
        ),
    )(
        lister,
        wanted,
        entry,
        own.reshape(IB, IMG, features),
        got.reshape(IB, IMG, features),
        own.reshape(TB, TXT, features),
        got.reshape(TB, TXT, features),
    )
    return grads.reshape(1, rows, features), stats.reshape(1, rows)


def solution(mesh):
    placed = (P("tower", "shard", None), P(), P())
    return jax.shard_map(
        body,
        mesh=mesh,
        in_specs=placed,
        out_specs=(P("tower", "shard", None), P("tower", "shard")),
        check_vma=False,
    )
```

```python
import functools
import math

import jax
import jax.numpy as jnp
from jax import lax
from jax.experimental import pallas as pl
from jax.experimental.pallas import tpu as pltpu
from jax.sharding import PartitionSpec as P

MESH = pl.DeviceIdType.MESH
TXT = 256
IMG = 128
TB = 8
IB = 16
SIDE = 4
CHIPS = 64
SLOTS = 32
GROUP = 4
STEP = 35
STEP_INV = 11
NT = (((1,), (1,)), ((), ()))
TN = (((0,), (0,)), ((), ()))


def hop_of(p):
    return lax.rem(p * STEP, CHIPS)


def moved(chip, hop, sign):
    div, rem = lax.div, lax.rem
    y = rem(div(chip, 16) + sign * div(hop, 16) + SIDE, SIDE)
    x = rem(rem(div(chip, 4), SIDE) + sign * rem(div(hop, 4), SIDE) + SIDE, SIDE)
    z = rem(rem(chip, SIDE) + sign * rem(hop, SIDE) + SIDE, SIDE)
    return y * 16 + x * 4 + z


def kernel(
    factor,
    lister_ref,
    wanted_ref,
    entry_ref,
    image_own,
    image_got,
    text_own,
    text_got,
    out_ref,
    stat_ref,
    ibuf,
    xbuf,
    recv,
    send,
    ret,
    escore,
    wbuf,
    mst,
    tg,
    img,
    acc,
    lse_ref,
    st,
    pst,
    mneg,
    mret,
    pmass,
    fs,
    fr,
    rs,
    rr,
    ms,
    mr,
    ts,
    tr,
    gs,
    gr,
    one,
):
    t = lax.axis_index("tower")
    s = lax.axis_index("shard")
    other = 1 - t

    def dev(tower, chip):
        return {"tower": tower, "shard": chip}

    def fwd(j):
        p = 2 * j + t
        return pltpu.make_async_remote_copy(
            src_ref=send.at[j],
            dst_ref=recv.at[j],
            send_sem=fs.at[j],
            recv_sem=fr.at[j],
            device_id=dev(t, moved(s, hop_of(p), 1)),
            device_id_type=MESH,
        )

    def back(j):
        p = 2 * j + t
        return pltpu.make_async_remote_copy(
            src_ref=send.at[j],
            dst_ref=ret.at[p],
            send_sem=rs.at[j],
            recv_sem=rr.at[p],
            device_id=dev(0, moved(s, hop_of(p), -1)),
            device_id_type=MESH,
        )

    def back_mass(j):
        p = 2 * j + t
        return pltpu.make_async_remote_copy(
            src_ref=mneg.at[j],
            dst_ref=mret.at[p],
            send_sem=ms.at[j],
            recv_sem=mr.at[p],
            device_id=dev(0, moved(s, hop_of(p), -1)),
            device_id_type=MESH,
        )

    def arrived(p):
        return pltpu.make_async_remote_copy(
            src_ref=ret.at[p],
            dst_ref=ret.at[p],
            send_sem=rs.at[0],
            recv_sem=rr.at[p],
            device_id=dev(1, s),
            device_id_type=MESH,
        )

    def arrived_mass(p):
        return pltpu.make_async_remote_copy(
            src_ref=mret.at[p],
            dst_ref=mret.at[p],
            send_sem=ms.at[0],
            recv_sem=mr.at[p],
            device_id=dev(1, s),
            device_id_type=MESH,
        )

    def give(src, dst, ssem, rsem):
        return pltpu.make_async_remote_copy(
            src_ref=src,
            dst_ref=dst,
            send_sem=ssem,
            recv_sem=rsem,
            device_id=dev(other, s),
            device_id_type=MESH,
        )

    def loads(image, words, act):
        getattr(pltpu.make_async_copy(image, ibuf, one.at[0]), act)()
        getattr(pltpu.make_async_copy(words, xbuf, one.at[1]), act)()

    barrier = pltpu.get_barrier_semaphore()

    @pl.when(t == 0)
    def _():
        loads(image_own, text_got, "start")
        recv[0] = jnp.zeros((IMG, recv.shape[2]), recv.dtype)
        ret[0] = jnp.zeros((IMG, ret.shape[2]), ret.dtype)
        mret[0] = jnp.zeros((1, IMG), mret.dtype)
        wbuf[0] = jnp.zeros((IMG, TXT), wbuf.dtype)

        def greet(p, carry):
            pl.semaphore_signal(
                barrier,
                inc=1,
                device_id=dev(lax.rem(p, 2), moved(s, hop_of(p), 1)),
                device_id_type=MESH,
            )
            return carry

        lax.fori_loop(1, CHIPS, greet, 0)

    @pl.when(t == 1)
    def _():
        loads(image_got, text_own, "start")

        def greet(j, carry):
            chip = moved(s, hop_of(2 * j + 1), 1)
            for tower in range(2):
                pl.semaphore_signal(
                    barrier, inc=1, device_id=dev(tower, chip), device_id_type=MESH
                )
            return carry

        lax.fori_loop(0, SLOTS, greet, 0)

    pl.semaphore_signal(barrier, inc=1, device_id=dev(other, s), device_id_type=MESH)

    @pl.when(t == 0)
    def _():
        loads(image_own, text_got, "wait")
        pl.semaphore_wait(barrier, 64)

    @pl.when(t == 1)
    def _():
        loads(image_got, text_own, "wait")
        pl.semaphore_wait(barrier, 65)

    def pack(j, carry):
        @pl.when(j < SLOTS)
        def _():
            chip = moved(s, hop_of(2 * j + t), 1)
            send[jnp.minimum(j, SLOTS - 1)] = ibuf[jnp.maximum(wanted_ref[chip], 0)]

        @pl.when(2 * j + t >= 3)
        def _():
            fwd(j - 1).start()

        return carry

    lax.fori_loop(0, SLOTS + 1, pack, 0)

    rows8 = lax.broadcasted_iota(jnp.int32, (TB, TXT), 0)
    sub = lax.broadcasted_iota(jnp.int32, (IMG, TXT), 0)
    lane = lax.broadcasted_iota(jnp.int32, (IMG, TXT), 1)
    on_diag = lane == sub + t * IMG

    def scores(keys, block):
        got = lax.dot_general(
            keys, xbuf[block], NT, preferred_element_type=jnp.float32
        )
        return got * factor

    def keep(slot, val):
        top = jnp.max(val, axis=0, keepdims=True)
        ex = jnp.exp(val - top)
        escore[slot] = ex
        mst[slot] = top
        return top, jnp.sum(ex, axis=0, keepdims=True)

    def positive(block, carry):
        big, total, diag = carry
        val = scores(ibuf[2 * block + t], block)
        top, part = keep(SLOTS + block, val)
        here = rows8 == block
        on = jnp.sum(jnp.where(on_diag, val, 0.0), axis=0, keepdims=True)
        return (
            jnp.where(here, top, big),
            jnp.where(here, part, total),
            jnp.where(here, on, diag),
        )

    zero = jnp.zeros((TB, TXT), jnp.float32)
    big, total, diag = lax.fori_loop(0, TB, positive, (zero, zero, zero))

    def listed(group, carry):
        big, total = carry
        got = []
        for k in range(GROUP):
            j = group * GROUP + k

            @pl.when(2 * j + t > 0)
            def _():
                fwd(j).wait_recv()

        for k in range(GROUP):
            j = group * GROUP + k
            block = lister_ref[moved(s, hop_of(2 * j + t), -1)]
            val = scores(recv[j], jnp.maximum(block, 0))
            got.append((block, *keep(j, val)))
        new = big
        for block, top, _ in got:
            new = jnp.where(rows8 == block, jnp.maximum(new, top), new)
        total = total * jnp.exp(big - new)
        for block, top, part in got:
            total += jnp.where(rows8 == block, part * jnp.exp(top - new), 0.0)
        return new, total

    big, total = lax.fori_loop(0, SLOTS // GROUP, listed, (big, total))

    st[0] = big
    st[1] = total
    st[2] = diag
    share = give(st, pst, one.at[4], one.at[5])
    share.start()
    share.wait()
    big_o = pst[0]
    new = jnp.maximum(big, big_o)
    lse = new + jnp.log(total * jnp.exp(big - new) + pst[1] * jnp.exp(big_o - new))
    lse_ref[...] = lse
    loss = lse - (diag + pst[2])

    ones = jnp.ones((8, TXT), jnp.bfloat16)

    def column_mass(weight):
        got = lax.dot_general(ones, weight, NT, preferred_element_type=jnp.float32)
        return got[0:1]

    def depart(j):
        back(j).start()
        back_mass(j).start()

    def answer(j, carry):
        fwd(j).wait_send()
        block = lister_ref[moved(s, hop_of(2 * j + t), -1)]
        held = jnp.maximum(block, 0)
        scale = jnp.exp(mst[j] - lse_ref[pl.ds(held, 1), :])
        scale = jnp.where(block >= 0, scale, 0.0)
        weight = (escore[j] * scale).astype(jnp.bfloat16)
        wbuf[j] = weight
        send[j] = jnp.dot(
            weight, xbuf[held], preferred_element_type=jnp.float32
        ).astype(jnp.bfloat16)
        mneg[j] = column_mass(weight)

        @pl.when(2 * j + t >= 3)
        def _():
            depart(j - 1)

        return carry

    lax.fori_loop(1 - t, SLOTS, answer, 0)

    def answer_own(block, carry):
        slot = SLOTS + block
        scale = jnp.exp(mst[slot] - lse_ref[pl.ds(block, 1), :])
        weight = (escore[slot] * scale).astype(jnp.bfloat16)
        wbuf[slot] = weight
        part = jnp.dot(weight, xbuf[block], preferred_element_type=jnp.float32)
        mine = xbuf[block, pl.ds(pl.multiple_of(t * IMG, IMG), IMG), :]
        img[2 * block + t] = part - mine.astype(jnp.float32)
        pmass[block + TB * t] = column_mass(weight)
        return carry

    depart(SLOTS - 1)
    lax.fori_loop(0, TB, answer_own, 0)

    def give_image(block):
        return give(
            img.at[2 * block + 1], img.at[2 * block + 1], gs.at[block], gr.at[block]
        )

    give_mass = give(pmass.at[pl.ds(TB, TB)], pmass.at[pl.ds(TB, TB)], one.at[6], one.at[7])

    @pl.when(t == 1)
    def _():
        for block in range(TB):
            give_image(block).start()
        give_mass.start()

    def text(block):
        acc[...] = lax.dot_general(
            wbuf[SLOTS + block], ibuf[2 * block + t], TN, preferred_element_type=jnp.float32
        )

        def add(k, carry):
            ws, ks = [], []
            for half in range(2):
                slot = entry_ref[block, 2 * k + half]
                at = jnp.maximum(slot, 0)
                w = wbuf[at]
                ws.append(jnp.where(slot >= 0, w, jnp.zeros_like(w)))
                ks.append(recv[at])
            acc[...] += lax.dot_general(
                jnp.concatenate(ws, axis=0),
                jnp.concatenate(ks, axis=0),
                TN,
                preferred_element_type=jnp.float32,
            )
            return carry

        lax.fori_loop(0, 6, add, 0)
        rows = pl.ds(pl.multiple_of(t * IMG, IMG), IMG)
        acc[rows, :] = acc[rows, :] - ibuf[2 * block + t].astype(jnp.float32)

    def give_text(block):
        return give(tg.at[block], tg.at[block], ts.at[block], tr.at[block])

    @pl.when(t == 0)
    def _():
        def run(block, carry):
            text(block)
            tg[block] = acc[...]

            @pl.when(block >= 1)
            def _():
                give_text(block - 1).start()

            return carry

        lax.fori_loop(0, TB, run, 0)

        for block in range(TB):
            give_image(block).wait_recv()
        give_text(TB - 1).start()
        give_mass.wait_recv()
        r = lax.broadcasted_iota(jnp.int32, (TXT, TXT), 0)
        c = lax.broadcasted_iota(jnp.int32, (TXT, TXT), 1)
        same_row = (r % IB) == (c % IB)
        c1 = lax.broadcasted_iota(jnp.int32, (1, TXT), 1)
        cp = lax.broadcasted_iota(jnp.int32, (1, CHIPS), 1)

        def wanted_at(p):
            return wanted_ref[moved(s, hop_of(p), 1)]


        for q in range(4):
            for k in range(16):
                if q + k > 0:
                    arrived(16 * q + k).wait_recv()
            blk16 = jnp.full((1, TXT), -1, jnp.int32)
            for k in range(16):
                blk16 = jnp.where(c1 // 16 == k, wanted_at(16 * q + k), blk16)
            pick = jnp.where(same_row & (r // IB == blk16), 1.0, 0.0).astype(
                jnp.bfloat16
            )

            def gather(g, carry):
                rows = pl.ds(pl.multiple_of(g * 16, 16), 16)
                part = ret[pl.ds(16 * q, 16), rows, :].reshape(TXT, ret.shape[2])
                got = jnp.dot(pick, part, preferred_element_type=jnp.float32)
                got = img[:, rows, :] + got.reshape(IB, 16, ret.shape[2])
                if q < 3:
                    img[:, rows, :] = got
                else:
                    out_ref[:, rows, :] = got.astype(jnp.bfloat16)
                return carry

            lax.fori_loop(0, 8, gather, 0)

        for p in range(1, CHIPS):
            arrived_mass(p).wait_recv()
        b = lax.broadcasted_iota(jnp.int32, (IB, CHIPS), 0)
        blocks = jnp.full((1, CHIPS), -1, jnp.int32)
        for p in range(CHIPS):
            blocks = jnp.where(cp == p, wanted_at(p), blocks)
        mass = jnp.dot(
            jnp.where(b == blocks, 1.0, 0.0).astype(jnp.bfloat16),
            mret[...].reshape(CHIPS, IMG).astype(jnp.bfloat16),
            preferred_element_type=jnp.float32,
        )
        stat_ref[...] = mass
        for block in range(TB):
            for half in range(2):
                at = 2 * block + half
                stat_ref[at : at + 1, :] += pmass[block + TB * half]
        for block in range(TB):
            give_text(block).wait_send()

    @pl.when(t == 1)
    def _():
        def run(block, carry):
            text(block)
            give_text(block).wait_recv()
            done = (acc[...] + tg[block]).astype(jnp.bfloat16)
            out_ref[pl.ds(2 * block, 2)] = done.reshape(2, IMG, done.shape[1])
            return carry

        lax.fori_loop(0, TB, run, 0)
        for block in range(TB):
            for half in range(2):
                at = 2 * block + half
                stat_ref[at : at + 1, :] = loss[
                    block : block + 1, half * IMG : (half + 1) * IMG
                ]
        for block in range(TB):
            give_image(block).wait_send()
        give_mass.wait_send()

    def drain(j, carry):
        back(j).wait_send()
        back_mass(j).wait_send()
        return carry

    lax.fori_loop(1 - t, SLOTS, drain, 0)


def body(embeds, pairs, counts):
    rows = embeds.shape[1]
    features = embeds.shape[2]
    slots = pairs.shape[1]
    t = lax.axis_index("tower")
    s = lax.axis_index("shard")
    listed = jnp.arange(slots, dtype=jnp.int32)[None, :] < counts[:, None]
    source = jnp.where(listed, pairs // IB, -1)
    local = pairs % IB

    hit = source.reshape(CHIPS, TB * slots) == s
    wanted = jnp.max(jnp.where(hit, local.reshape(CHIPS, TB * slots), -1), axis=1)
    mine = lax.dynamic_slice_in_dim(source, s * TB, TB, 0)
    chips = jnp.arange(CHIPS, dtype=jnp.int32)
    block = lax.broadcasted_iota(jnp.int32, (CHIPS, TB, slots), 1)
    lister = jnp.max(
        jnp.where(mine[None] == chips[:, None, None], block, -1), axis=(1, 2)
    )
    hop = (
        ((s // 16 - mine // 16) % SIDE) * 16
        + ((s // 4 - mine // 4) % SIDE) * 4
        + (s - mine) % SIDE
    )
    step = (hop * STEP_INV) % CHIPS
    entry = jnp.where((mine >= 0) & (step % 2 == t), step // 2, -1)
    smem = pl.BlockSpec(memory_space=pltpu.SMEM)
    vmem = pl.BlockSpec(memory_space=pltpu.VMEM)
    bf16, f32 = jnp.bfloat16, jnp.float32
    own = embeds[0]
    got = lax.ppermute(own, "tower", [(0, 1), (1, 0)])
    dma = pltpu.SemaphoreType.DMA
    grads, stats = pl.pallas_call(
        functools.partial(kernel, 3.0 / math.sqrt(features)),
        out_shape=(
            pltpu.VMEM((IB, IMG, features), bf16),
            pltpu.VMEM((IB, IMG), f32),
        ),
        in_specs=[smem] * 3 + [pl.BlockSpec(memory_space=pl.ANY)] * 4,
        out_specs=(vmem, vmem),
        scratch_shapes=[
            pltpu.VMEM((IB, IMG, features), bf16),
            pltpu.VMEM((TB, TXT, features), bf16),
            pltpu.VMEM((SLOTS, IMG, features), bf16),
            pltpu.VMEM((SLOTS, IMG, features), bf16),
            pltpu.VMEM((CHIPS, IMG, features), bf16),
            pltpu.VMEM((SLOTS + TB, IMG, TXT), f32),
            pltpu.VMEM((SLOTS + TB, IMG, TXT), bf16),
            pltpu.VMEM((SLOTS + TB, 1, TXT), f32),
            pltpu.VMEM((TB, TXT, features), f32),
            pltpu.VMEM((IB, IMG, features), f32),
            pltpu.VMEM((TXT, features), f32),
            pltpu.VMEM((TB, TXT), f32),
            pltpu.VMEM((3, TB, TXT), f32),
            pltpu.VMEM((3, TB, TXT), f32),
            pltpu.VMEM((SLOTS, 1, IMG), f32),
            pltpu.VMEM((CHIPS, 1, IMG), f32),
            pltpu.VMEM((2 * TB, 1, IMG), f32),
            dma((SLOTS,)),
            dma((SLOTS,)),
            dma((SLOTS,)),
            dma((CHIPS,)),
            dma((SLOTS,)),
            dma((CHIPS,)),
            dma((TB,)),
            dma((TB,)),
            dma((TB,)),
            dma((TB,)),
            dma((8,)),
        ],
        compiler_params=pltpu.CompilerParams(
            collective_id=0, has_side_effects=True, vmem_limit_bytes=58_500_000
        ),
    )(
        lister,
        wanted,
        entry,
        own.reshape(IB, IMG, features),
        got.reshape(IB, IMG, features),
        own.reshape(TB, TXT, features),
        got.reshape(TB, TXT, features),
    )
    return grads.reshape(1, rows, features), stats.reshape(1, rows)


def solution(mesh):
    placed = (P("tower", "shard", None), P(), P())
    return jax.shard_map(
        body,
        mesh=mesh,
        in_specs=placed,
        out_specs=(P("tower", "shard", None), P("tower", "shard")),
        check_vma=False,
    )
```

```python
import functools
import math

import jax
import jax.numpy as jnp
from jax import lax
from jax.experimental import pallas as pl
from jax.experimental.pallas import tpu as pltpu
from jax.sharding import PartitionSpec as P

MESH = pl.DeviceIdType.MESH
TXT = 256
IMG = 128
TB = 8
IB = 16
SIDE = 4
CHIPS = 64
SLOTS = 32
GROUP = 4
STEP = 35
STEP_INV = 11
NT = (((1,), (1,)), ((), ()))
TN = (((0,), (0,)), ((), ()))


def hop_of(p):
    return lax.rem(p * STEP, CHIPS)


def moved(chip, hop, sign):
    div, rem = lax.div, lax.rem
    y = rem(div(chip, 16) + sign * div(hop, 16) + SIDE, SIDE)
    x = rem(rem(div(chip, 4), SIDE) + sign * rem(div(hop, 4), SIDE) + SIDE, SIDE)
    z = rem(rem(chip, SIDE) + sign * rem(hop, SIDE) + SIDE, SIDE)
    return y * 16 + x * 4 + z


def kernel(
    factor,
    lister_ref,
    wanted_ref,
    entry_ref,
    image_own,
    image_got,
    text_own,
    text_got,
    out_ref,
    stat_ref,
    ibuf,
    xbuf,
    recv,
    send,
    ret,
    escore,
    wbuf,
    mst,
    tg,
    img,
    acc,
    lse_ref,
    st,
    pst,
    mneg,
    mret,
    pmass,
    fs,
    fr,
    rs,
    rr,
    ms,
    mr,
    ts,
    tr,
    gs,
    gr,
    one,
):
    t = lax.axis_index("tower")
    s = lax.axis_index("shard")
    other = 1 - t

    def dev(tower, chip):
        return {"tower": tower, "shard": chip}

    def fwd(j):
        p = 2 * j + t
        return pltpu.make_async_remote_copy(
            src_ref=send.at[j],
            dst_ref=recv.at[j],
            send_sem=fs.at[j],
            recv_sem=fr.at[j],
            device_id=dev(t, moved(s, hop_of(p), 1)),
            device_id_type=MESH,
        )

    def back(j):
        p = 2 * j + t
        return pltpu.make_async_remote_copy(
            src_ref=send.at[j],
            dst_ref=ret.at[p],
            send_sem=rs.at[j],
            recv_sem=rr.at[p],
            device_id=dev(0, moved(s, hop_of(p), -1)),
            device_id_type=MESH,
        )

    def back_mass(j):
        p = 2 * j + t
        return pltpu.make_async_remote_copy(
            src_ref=mneg.at[j],
            dst_ref=mret.at[p],
            send_sem=ms.at[j],
            recv_sem=mr.at[p],
            device_id=dev(0, moved(s, hop_of(p), -1)),
            device_id_type=MESH,
        )

    def arrived(p):
        return pltpu.make_async_remote_copy(
            src_ref=ret.at[p],
            dst_ref=ret.at[p],
            send_sem=rs.at[0],
            recv_sem=rr.at[p],
            device_id=dev(1, s),
            device_id_type=MESH,
        )

    def arrived_mass(p):
        return pltpu.make_async_remote_copy(
            src_ref=mret.at[p],
            dst_ref=mret.at[p],
            send_sem=ms.at[0],
            recv_sem=mr.at[p],
            device_id=dev(1, s),
            device_id_type=MESH,
        )

    def give(src, dst, ssem, rsem):
        return pltpu.make_async_remote_copy(
            src_ref=src,
            dst_ref=dst,
            send_sem=ssem,
            recv_sem=rsem,
            device_id=dev(other, s),
            device_id_type=MESH,
        )

    def loads(image, words, act):
        getattr(pltpu.make_async_copy(image, ibuf, one.at[0]), act)()
        getattr(pltpu.make_async_copy(words, xbuf, one.at[1]), act)()

    barrier = pltpu.get_barrier_semaphore()

    @pl.when(t == 0)
    def _():
        loads(image_own, text_got, "start")
        recv[0] = jnp.zeros((IMG, recv.shape[2]), recv.dtype)
        ret[0] = jnp.zeros((IMG, ret.shape[2]), ret.dtype)
        mret[0] = jnp.zeros((1, IMG), mret.dtype)
        wbuf[0] = jnp.zeros((IMG, TXT), wbuf.dtype)

        def greet(p, carry):
            pl.semaphore_signal(
                barrier,
                inc=1,
                device_id=dev(lax.rem(p, 2), moved(s, hop_of(p), 1)),
                device_id_type=MESH,
            )
            return carry

        lax.fori_loop(1, CHIPS, greet, 0)

    @pl.when(t == 1)
    def _():
        loads(image_got, text_own, "start")

        def greet(j, carry):
            chip = moved(s, hop_of(2 * j + 1), 1)
            for tower in range(2):
                pl.semaphore_signal(
                    barrier, inc=1, device_id=dev(tower, chip), device_id_type=MESH
                )
            return carry

        lax.fori_loop(0, SLOTS, greet, 0)

    pl.semaphore_signal(barrier, inc=1, device_id=dev(other, s), device_id_type=MESH)

    @pl.when(t == 0)
    def _():
        loads(image_own, text_got, "wait")
        pl.semaphore_wait(barrier, 64)

    @pl.when(t == 1)
    def _():
        loads(image_got, text_own, "wait")
        pl.semaphore_wait(barrier, 65)

    def pack(j, carry):
        @pl.when(j < SLOTS)
        def _():
            chip = moved(s, hop_of(2 * j + t), 1)
            send[jnp.minimum(j, SLOTS - 1)] = ibuf[jnp.maximum(wanted_ref[chip], 0)]

        @pl.when(2 * j + t >= 3)
        def _():
            fwd(j - 1).start()

        return carry

    lax.fori_loop(0, SLOTS + 1, pack, 0)

    rows8 = lax.broadcasted_iota(jnp.int32, (TB, TXT), 0)
    sub = lax.broadcasted_iota(jnp.int32, (IMG, TXT), 0)
    lane = lax.broadcasted_iota(jnp.int32, (IMG, TXT), 1)
    on_diag = lane == sub + t * IMG

    def scores(keys, block):
        got = lax.dot_general(
            keys, xbuf[block], NT, preferred_element_type=jnp.float32
        )
        return got * factor

    def keep(slot, val):
        top = jnp.max(val, axis=0, keepdims=True)
        ex = jnp.exp(val - top)
        escore[slot] = ex
        mst[slot] = top
        return top, jnp.sum(ex, axis=0, keepdims=True)

    def positive(block, carry):
        big, total, diag = carry
        val = scores(ibuf[2 * block + t], block)
        top, part = keep(SLOTS + block, val)
        here = rows8 == block
        on = jnp.sum(jnp.where(on_diag, val, 0.0), axis=0, keepdims=True)
        return (
            jnp.where(here, top, big),
            jnp.where(here, part, total),
            jnp.where(here, on, diag),
        )

    zero = jnp.zeros((TB, TXT), jnp.float32)
    big, total, diag = lax.fori_loop(0, TB, positive, (zero, zero, zero))

    def listed(group, carry):
        big, total = carry
        got = []
        for k in range(GROUP):
            j = group * GROUP + k

            @pl.when(2 * j + t > 0)
            def _():
                fwd(j).wait_recv()

        for k in range(GROUP):
            j = group * GROUP + k
            block = lister_ref[moved(s, hop_of(2 * j + t), -1)]
            val = scores(recv[j], jnp.maximum(block, 0))
            got.append((block, *keep(j, val)))
        new = big
        for block, top, _ in got:
            new = jnp.where(rows8 == block, jnp.maximum(new, top), new)
        total = total * jnp.exp(big - new)
        for block, top, part in got:
            total += jnp.where(rows8 == block, part * jnp.exp(top - new), 0.0)
        return new, total

    big, total = lax.fori_loop(0, SLOTS // GROUP, listed, (big, total))

    st[0] = big
    st[1] = total
    st[2] = diag
    share = give(st, pst, one.at[4], one.at[5])
    share.start()
    share.wait()
    big_o = pst[0]
    new = jnp.maximum(big, big_o)
    lse = new + jnp.log(total * jnp.exp(big - new) + pst[1] * jnp.exp(big_o - new))
    lse_ref[...] = lse
    loss = lse - (diag + pst[2])

    ones = jnp.ones((8, TXT), jnp.bfloat16)

    def column_mass(weight):
        got = lax.dot_general(ones, weight, NT, preferred_element_type=jnp.float32)
        return got[0:1]

    def depart(j):
        back(j).start()
        back_mass(j).start()

    def answer(j, carry):
        fwd(j).wait_send()
        block = lister_ref[moved(s, hop_of(2 * j + t), -1)]
        held = jnp.maximum(block, 0)
        scale = jnp.exp(mst[j] - lse_ref[pl.ds(held, 1), :])
        scale = jnp.where(block >= 0, scale, 0.0)
        weight = (escore[j] * scale).astype(jnp.bfloat16)
        wbuf[j] = weight
        send[j] = jnp.dot(
            weight, xbuf[held], preferred_element_type=jnp.float32
        ).astype(jnp.bfloat16)
        mneg[j] = column_mass(weight)

        @pl.when(2 * j + t >= 3)
        def _():
            depart(j - 1)

        return carry

    lax.fori_loop(1 - t, SLOTS, answer, 0)

    def answer_own(block, carry):
        slot = SLOTS + block
        scale = jnp.exp(mst[slot] - lse_ref[pl.ds(block, 1), :])
        weight = (escore[slot] * scale).astype(jnp.bfloat16)
        wbuf[slot] = weight
        part = jnp.dot(weight, xbuf[block], preferred_element_type=jnp.float32)
        mine = xbuf[block, pl.ds(pl.multiple_of(t * IMG, IMG), IMG), :]
        img[2 * block + t] = part - mine.astype(jnp.float32)
        pmass[block + TB * t] = column_mass(weight)
        return carry

    depart(SLOTS - 1)
    lax.fori_loop(0, TB, answer_own, 0)

    def give_image(block):
        return give(
            img.at[2 * block + 1], img.at[2 * block + 1], gs.at[block], gr.at[block]
        )

    give_mass = give(pmass.at[pl.ds(TB, TB)], pmass.at[pl.ds(TB, TB)], one.at[6], one.at[7])

    @pl.when(t == 1)
    def _():
        for block in range(TB):
            give_image(block).start()
        give_mass.start()

    def text(block):
        acc[...] = lax.dot_general(
            wbuf[SLOTS + block], ibuf[2 * block + t], TN, preferred_element_type=jnp.float32
        )

        def add(k, carry):
            ws, ks = [], []
            for half in range(2):
                slot = entry_ref[block, 2 * k + half]
                at = jnp.maximum(slot, 0)
                w = wbuf[at]
                ws.append(jnp.where(slot >= 0, w, jnp.zeros_like(w)))
                ks.append(recv[at])
            acc[...] += lax.dot_general(
                jnp.concatenate(ws, axis=0),
                jnp.concatenate(ks, axis=0),
                TN,
                preferred_element_type=jnp.float32,
            )
            return carry

        lax.fori_loop(0, 6, add, 0)
        rows = pl.ds(pl.multiple_of(t * IMG, IMG), IMG)
        acc[rows, :] = acc[rows, :] - ibuf[2 * block + t].astype(jnp.float32)

    def give_text(block):
        return give(tg.at[block], tg.at[block], ts.at[block], tr.at[block])

    @pl.when(t == 0)
    def _():
        def run(block, carry):
            text(block)
            tg[block] = acc[...]

            @pl.when(block >= 1)
            def _():
                give_text(block - 1).start()

            return carry

        lax.fori_loop(0, TB, run, 0)

        for block in range(TB):
            give_image(block).wait_recv()
        give_text(TB - 1).start()
        give_mass.wait_recv()
        r = lax.broadcasted_iota(jnp.int32, (TXT, TXT), 0)
        c = lax.broadcasted_iota(jnp.int32, (TXT, TXT), 1)
        same_row = (r % IB) == (c % IB)
        c1 = lax.broadcasted_iota(jnp.int32, (1, TXT), 1)
        cp = lax.broadcasted_iota(jnp.int32, (1, CHIPS), 1)

        def wanted_at(p):
            return wanted_ref[moved(s, hop_of(p), 1)]


        b = lax.broadcasted_iota(jnp.int32, (IB, CHIPS), 0)
        blocks = jnp.full((1, CHIPS), -1, jnp.int32)
        for p in range(CHIPS):
            blocks = jnp.where(cp == p, wanted_at(p), blocks)

        for q in range(4):
            blk16 = jnp.full((1, TXT), -1, jnp.int32)
            for k in range(16):
                blk16 = jnp.where(c1 // 16 == k, wanted_at(16 * q + k), blk16)
            pick = jnp.where(same_row & (r // IB == blk16), 1.0, 0.0).astype(
                jnp.bfloat16
            )
            for k in range(16):
                if q + k > 0:
                    arrived(16 * q + k).wait_recv()

            def gather(g, carry):
                rows = pl.ds(pl.multiple_of(g * 16, 16), 16)
                part = ret[pl.ds(16 * q, 16), rows, :].reshape(TXT, ret.shape[2])
                got = jnp.dot(pick, part, preferred_element_type=jnp.float32)
                got = img[:, rows, :] + got.reshape(IB, 16, ret.shape[2])
                if q < 3:
                    img[:, rows, :] = got
                else:
                    out_ref[:, rows, :] = got.astype(jnp.bfloat16)
                return carry

            lax.fori_loop(0, 8, gather, 0)

        for p in range(1, CHIPS):
            arrived_mass(p).wait_recv()
        mass = jnp.dot(
            jnp.where(b == blocks, 1.0, 0.0).astype(jnp.bfloat16),
            mret[...].reshape(CHIPS, IMG).astype(jnp.bfloat16),
            preferred_element_type=jnp.float32,
        )
        stat_ref[...] = mass
        for block in range(TB):
            for half in range(2):
                at = 2 * block + half
                stat_ref[at : at + 1, :] += pmass[block + TB * half]
        for block in range(TB):
            give_text(block).wait_send()

    @pl.when(t == 1)
    def _():
        def run(block, carry):
            text(block)
            give_text(block).wait_recv()
            done = (acc[...] + tg[block]).astype(jnp.bfloat16)
            out_ref[pl.ds(2 * block, 2)] = done.reshape(2, IMG, done.shape[1])
            return carry

        lax.fori_loop(0, TB, run, 0)
        for block in range(TB):
            for half in range(2):
                at = 2 * block + half
                stat_ref[at : at + 1, :] = loss[
                    block : block + 1, half * IMG : (half + 1) * IMG
                ]
        for block in range(TB):
            give_image(block).wait_send()
        give_mass.wait_send()

    def drain(j, carry):
        back(j).wait_send()
        back_mass(j).wait_send()
        return carry

    lax.fori_loop(1 - t, SLOTS, drain, 0)


def body(embeds, pairs, counts):
    rows = embeds.shape[1]
    features = embeds.shape[2]
    slots = pairs.shape[1]
    t = lax.axis_index("tower")
    s = lax.axis_index("shard")
    listed = jnp.arange(slots, dtype=jnp.int32)[None, :] < counts[:, None]
    source = jnp.where(listed, pairs // IB, -1)
    local = pairs % IB

    hit = source.reshape(CHIPS, TB * slots) == s
    wanted = jnp.max(jnp.where(hit, local.reshape(CHIPS, TB * slots), -1), axis=1)
    mine = lax.dynamic_slice_in_dim(source, s * TB, TB, 0)
    chips = jnp.arange(CHIPS, dtype=jnp.int32)
    block = lax.broadcasted_iota(jnp.int32, (CHIPS, TB, slots), 1)
    lister = jnp.max(
        jnp.where(mine[None] == chips[:, None, None], block, -1), axis=(1, 2)
    )
    hop = (
        ((s // 16 - mine // 16) % SIDE) * 16
        + ((s // 4 - mine // 4) % SIDE) * 4
        + (s - mine) % SIDE
    )
    step = (hop * STEP_INV) % CHIPS
    entry = jnp.where((mine >= 0) & (step % 2 == t), step // 2, -1)
    smem = pl.BlockSpec(memory_space=pltpu.SMEM)
    vmem = pl.BlockSpec(memory_space=pltpu.VMEM)
    bf16, f32 = jnp.bfloat16, jnp.float32
    own = embeds[0]
    got = lax.ppermute(own, "tower", [(0, 1), (1, 0)])
    dma = pltpu.SemaphoreType.DMA
    grads, stats = pl.pallas_call(
        functools.partial(kernel, 3.0 / math.sqrt(features)),
        out_shape=(
            pltpu.VMEM((IB, IMG, features), bf16),
            pltpu.VMEM((IB, IMG), f32),
        ),
        in_specs=[smem] * 3 + [pl.BlockSpec(memory_space=pl.ANY)] * 4,
        out_specs=(vmem, vmem),
        scratch_shapes=[
            pltpu.VMEM((IB, IMG, features), bf16),
            pltpu.VMEM((TB, TXT, features), bf16),
            pltpu.VMEM((SLOTS, IMG, features), bf16),
            pltpu.VMEM((SLOTS, IMG, features), bf16),
            pltpu.VMEM((CHIPS, IMG, features), bf16),
            pltpu.VMEM((SLOTS + TB, IMG, TXT), f32),
            pltpu.VMEM((SLOTS + TB, IMG, TXT), bf16),
            pltpu.VMEM((SLOTS + TB, 1, TXT), f32),
            pltpu.VMEM((TB, TXT, features), f32),
            pltpu.VMEM((IB, IMG, features), f32),
            pltpu.VMEM((TXT, features), f32),
            pltpu.VMEM((TB, TXT), f32),
            pltpu.VMEM((3, TB, TXT), f32),
            pltpu.VMEM((3, TB, TXT), f32),
            pltpu.VMEM((SLOTS, 1, IMG), f32),
            pltpu.VMEM((CHIPS, 1, IMG), f32),
            pltpu.VMEM((2 * TB, 1, IMG), f32),
            dma((SLOTS,)),
            dma((SLOTS,)),
            dma((SLOTS,)),
            dma((CHIPS,)),
            dma((SLOTS,)),
            dma((CHIPS,)),
            dma((TB,)),
            dma((TB,)),
            dma((TB,)),
            dma((TB,)),
            dma((8,)),
        ],
        compiler_params=pltpu.CompilerParams(
            collective_id=0, has_side_effects=True, vmem_limit_bytes=58_500_000
        ),
    )(
        lister,
        wanted,
        entry,
        own.reshape(IB, IMG, features),
        got.reshape(IB, IMG, features),
        own.reshape(TB, TXT, features),
        got.reshape(TB, TXT, features),
    )
    return grads.reshape(1, rows, features), stats.reshape(1, rows)


def solution(mesh):
    placed = (P("tower", "shard", None), P(), P())
    return jax.shard_map(
        body,
        mesh=mesh,
        in_specs=placed,
        out_specs=(P("tower", "shard", None), P("tower", "shard")),
        check_vma=False,
    )
```
